512 devices in a mesh: seq: 32 (over y, x), chan: 16 (over z, core).
Axes of the slice: x: 4, y: 8, z: 8, core: 2. Of those that a mesh axis runs over, the one named last changes fastest.
Arguments:
- tokens: bfloat16 [8192, 2048], P(('seq', 'chan')), may hold values from -6 to 6
- norm_gain: float32 [2048], replicated, may hold values from 0.1 to 1.9
- entry_projection_matrix: bfloat16 [2, 2048, 4096], P(None, None, 'chan'), may hold values from -0.125 to 0.125
- conv_weight: float32 [4, 4096], P(None, 'chan'), may hold values from -3 to 3
- conv_bias: float32 [4096], P('chan'), may hold values from -3 to 3
- w_x: bfloat16 [4096, 160], P('chan'), may hold values from -0.09375 to 0.09375
- timescale_matrix: bfloat16 [128, 4096], P(None, 'chan'), may hold values from -0.5 to 0.5
- timescale_offset: float32 [4096], P('chan'), may hold values from -8 to -2
- a_log: float32 [16, 4096], P(None, 'chan'), may hold values from -1 to 2.77
- skip_gain: float32 [4096], P('chan'), may hold values from 0.5 to 1.5
- w_out: bfloat16 [4096, 2048], P('chan'), may hold values from -0.09375 to 0.09375
- lengths: int32 [4], replicated, may hold values from 1 to 4096, 7936 in all
- req_order: int32 [4], replicated, may hold values from 0 to 3, each once
Outputs:
- mixed: bfloat16 [8192, 2048], P(('seq', 'chan'))
- last_states: float32 [4, 16, 4096], P(None, None, ('chan', 'seq'))
- conv_edges: bfloat16 [4, 4, 4096], P(None, None, ('chan', 'seq'))
The draws below stay inside these ranges and needn't reach their ends.
Inputs may be any that keep to these rules, and one draw needn't show every extreme that they name: The lengths sum to exactly 7936, and the longest is exactly 4096. `req_order`: each request appears exactly once.
All inputs are finite; a program needn't handle non-finite values.
Results may differ from the reference program's by a relative error of at most 0.0095.
Values may be sent and summed in bfloat16 or wider, within the bound.
No kernel may reach another device: no remote copies, remote signals or barrier semaphores. Data moves between devices by JAX's collectives and lax.ppermute only.
A program may use at most 64 MiB of HBM per device.

```python
import math
import jax
import jax.numpy as jnp
import numpy as np
from jax import lax

D = 2048
E = 4096
NSTATE = 16
RANK = 128
KCONV = 4
STRETCH = 64
REQS = 4
TOKENS = 8192
MOST = 4096


def steps_of(own_key, shape, cuts, low, high):
    level = 1.0
    for position, blocks in cuts:
        draws = jax.random.uniform(jax.random.fold_in(jax.random.fold_in(own_key, 6), position), (blocks,), jnp.float32, low / len(cuts), high / len(cuts))
        level = level * jnp.repeat(jnp.exp(draws), shape[position] // blocks).reshape((-1,) + (1,) * (len(shape) - 1 - position))
    return level


def length_profile(number_of, total, limit, lean):
    weights = [(1 << 20) // math.isqrt(standing ** lean) + 1 for standing in range(2, number_of + 1)]
    rest, counts = total - limit - (number_of - 1), [1] * (number_of - 1)
    while rest > 0:
        free = [i for i in range(number_of - 1) if counts[i] < limit]
        whole, remaining = sum([weights[i] for i in free]), rest
        for i in free:
            more = min(limit - counts[i], max(1, remaining * weights[i] // whole), rest)
            counts[i] = counts[i] + more
            rest = rest - more
    return np.array([limit] + counts)


def uneven(rng, number_of, total, limit, lean):
    if number_of == 2:
        one = jax.random.randint(rng, (), max(1, total - limit), min(limit, total - 1) + 1)
        return jnp.stack([one, total - one])
    sizes = jnp.asarray(length_profile(number_of, total, limit, lean), jnp.int32)
    pairs = (number_of - 1) // 2
    donor, receiver = sizes[1:1 + 2 * pairs:2], sizes[2:2 + 2 * pairs:2]
    slack = jnp.minimum(donor - 1, limit - receiver)
    passed = jax.random.randint(jax.random.fold_in(rng, 1), (pairs,), 0, 1 << 20) % (slack + 1)
    sizes = sizes.at[1:1 + 2 * pairs:2].set(donor - passed).at[2:2 + 2 * pairs:2].set(receiver + passed)
    return sizes[jax.random.permutation(jax.random.fold_in(rng, 2), number_of)]


def noise(rng, shape, width, most, pieces=(), kind=jnp.bfloat16):
    gain = steps_of(rng, shape, pieces, -0.22, 0.18) if pieces else 1.0
    result = jax.random.normal(rng, shape, jnp.float32) * width * gain
    return jnp.minimum(jnp.maximum(result, -most), most).astype(kind)


def setup_inputs(seed: int = 0) -> dict:
    key_of = jax.random.split(jax.random.key(seed), 14)
    tokens = noise(key_of[0], (TOKENS, D), 1.0, 6.0, ((0, 512),))
    norm_gain = jnp.clip(1.0 + 0.18 * jax.random.normal(key_of[1], (D,), jnp.float32), 0.1, 1.9)
    entry_projection_matrix = noise(key_of[2], (2, D, E), D ** -0.5, 0.125, ((2, 16),))
    conv_weight = noise(key_of[3], (KCONV, E), 0.5, 3.0, ((1, 16),), jnp.float32)
    conv_bias = noise(key_of[4], (E,), 0.5, 3.0, ((0, 16),), jnp.float32)
    w_x = noise(key_of[5], (E, RANK + 2 * NSTATE), E ** -0.5, 0.09375, ((0, 16),))
    timescale_matrix = noise(key_of[6], (RANK, E), RANK ** -0.5, 0.5, ((1, 16),))
    timescale_offset = jnp.clip(-8.0 + 6.0 * jax.random.uniform(key_of[7], (E,), jnp.float32) ** steps_of(key_of[7], (E,), ((0, 16),), -0.2, 0.2), -8.0, -2.0)
    a_log = jnp.clip(-1.0 + 3.77 * jax.random.uniform(key_of[8], (NSTATE, E), jnp.float32) ** steps_of(key_of[8], (NSTATE, E), ((1, 16),), -0.2, 0.2), -1.0, 2.77)
    skip_gain = jnp.clip(0.5 + 1.0 * jax.random.uniform(key_of[9], (E,), jnp.float32) ** steps_of(key_of[9], (E,), ((0, 16),), -0.2, 0.2), 0.5, 1.5)
    w_out = noise(key_of[10], (E, D), E ** -0.5, 0.09375, ((0, 16),))
    lengths = uneven(key_of[11], REQS, TOKENS - REQS * STRETCH, MOST, 2).astype(jnp.int32)
    req_order = jax.random.permutation(key_of[12], REQS).astype(jnp.int32)
    return dict(tokens=tokens, norm_gain=norm_gain, entry_projection_matrix=entry_projection_matrix, conv_weight=conv_weight, conv_bias=conv_bias, w_x=w_x, timescale_matrix=timescale_matrix, timescale_offset=timescale_offset, a_log=a_log, skip_gain=skip_gain, w_out=w_out, lengths=lengths, req_order=req_order)


def sequence_arrangement(lengths, req_order, slot_ids):
    req_count = lengths.shape[0]
    req_index = jnp.arange(req_count, dtype=jnp.int32)
    filled_length_total = ((lengths + STRETCH - 1) // STRETCH * STRETCH).astype(jnp.int32)
    pick_order = (req_order[:, None] == req_index[None, :]).astype(jnp.int32)
    placed_pad = lax.optimization_barrier(jnp.sum(pick_order * filled_length_total[None, :], axis=1)).astype(jnp.int32)
    placed_len = lax.optimization_barrier(jnp.sum(pick_order * lengths[None, :], axis=1)).astype(jnp.int32)
    end_slots = jnp.cumsum(placed_pad).astype(jnp.int32)
    begin_slots = (end_slots - placed_pad).astype(jnp.int32)
    sequence_beginnings = lax.optimization_barrier(jnp.sum(pick_order * begin_slots[:, None], axis=0)).astype(jnp.int32)
    inside = (slot_ids[:, None] >= begin_slots[None, :]) & (slot_ids[:, None] < end_slots[None, :])
    slot_owner = lax.optimization_barrier(jnp.sum(jnp.where(inside, req_index[None, :] + 1, 0), axis=1)).astype(jnp.int32)
    slot_owner = jnp.where(slot_ids < 0, -1, slot_owner).astype(jnp.int32)
    in_request = inside & (slot_ids[:, None] - begin_slots[None, :] < placed_len[None, :])
    present_flag = lax.optimization_barrier(jnp.sum(jnp.where(in_request, 1, 0), axis=1)).astype(jnp.int32)
    return (filled_length_total, sequence_beginnings, slot_owner, present_flag)

def reference(tokens, norm_gain, entry_projection_matrix, conv_weight, conv_bias, w_x, timescale_matrix, timescale_offset, a_log, skip_gain, w_out, lengths, req_order):
    slot_ids = jnp.arange(TOKENS, dtype=jnp.int32)
    filled_length_total, sequence_beginnings, slot_owner, present_flag = sequence_arrangement(lengths, req_order, slot_ids)
    position_presence = present_flag.astype(jnp.float32)
    widened = tokens.astype(jnp.float32)
    scale_row = lax.rsqrt(lax.optimization_barrier(jnp.mean(widened * widened, axis=1, keepdims=True)) + 1e-05)
    rescaled_entries = (widened * scale_row * norm_gain[None, :]).astype(jnp.bfloat16)
    mixer_signal = (jnp.dot(rescaled_entries, entry_projection_matrix[0], preferred_element_type=jnp.float32) * position_presence[:, None]).astype(jnp.bfloat16)
    switch_signal = jnp.dot(rescaled_entries, entry_projection_matrix[1], preferred_element_type=jnp.float32).astype(jnp.bfloat16)
    inner_wide = mixer_signal.astype(jnp.float32)
    conv_sum = conv_bias[None, :] + conv_weight[KCONV - 1][None, :] * inner_wide
    for shift_by in range(1, KCONV):
        moved = jnp.pad(inner_wide, ((shift_by, 0), (0, 0)))[:TOKENS]
        prior_owner = jnp.pad(slot_owner, (shift_by, 0), constant_values=-1)[:TOKENS]
        same_req = (prior_owner == slot_owner).astype(jnp.float32)
        conv_sum = conv_sum + conv_weight[KCONV - 1 - shift_by][None, :] * moved * same_req[:, None]
    activated = jax.nn.silu(conv_sum).astype(jnp.bfloat16)
    x_proj = jnp.dot(activated, w_x, preferred_element_type=jnp.float32)
    thin_timescale_factor = x_proj[:, :RANK].astype(jnp.bfloat16)
    in_coef = x_proj[:, RANK:RANK + NSTATE]
    out_coef = x_proj[:, RANK + NSTATE:]
    timescale_values = position_presence[:, None] * jax.nn.softplus(jnp.dot(thin_timescale_factor, timescale_matrix, preferred_element_type=jnp.float32) + timescale_offset[None, :])
    decay_rate = -jnp.exp(a_log)
    prior_owner = jnp.pad(slot_owner, (1, 0), constant_values=-1)[:TOKENS]
    keep_flag = (prior_owner == slot_owner).astype(jnp.float32)
    act_wide = activated.astype(jnp.float32)
    stretch_count = TOKENS // STRETCH

    def per_slot(state_now, slot_in):
        step_delta, step_input, step_in, step_out, step_keep = slot_in
        state_now = step_keep * jnp.exp(step_delta[None, :] * decay_rate) * state_now + (step_delta * step_input)[None, :] * step_in[:, None]
        return (state_now, lax.optimization_barrier(jnp.sum(step_out[:, None] * state_now, axis=0)))

    def per_stretch(state_now, stretch_in):
        state_now, outputs = lax.scan(per_slot, state_now, stretch_in)
        return (state_now, (outputs, state_now))

    def by_stretch(values):
        return values.reshape((stretch_count, STRETCH) + values.shape[1:])
    initial = jnp.zeros((NSTATE, E), jnp.float32)
    stretch_in = (by_stretch(timescale_values), by_stretch(act_wide), by_stretch(in_coef), by_stretch(out_coef), by_stretch(keep_flag))
    final_state, (outputs, stretch_ends) = lax.scan(per_stretch, initial, stretch_in)
    complete_result = outputs.reshape(TOKENS, E) + skip_gain[None, :] * act_wide
    switched_result = (position_presence[:, None] * complete_result * jax.nn.silu(switch_signal.astype(jnp.float32))).astype(jnp.bfloat16)
    mixed = (widened + jnp.dot(switched_result, w_out, preferred_element_type=jnp.float32)).astype(jnp.bfloat16)
    last_stretch = ((sequence_beginnings + filled_length_total) // STRETCH - 1).astype(jnp.int32)
    last_states = stretch_ends[last_stretch]
    offsets = jnp.arange(KCONV, dtype=jnp.int32)
    back_pos = (lengths[:, None] - KCONV + offsets[None, :]).astype(jnp.int32)
    target = jnp.clip(sequence_beginnings[:, None] + back_pos, 0, TOKENS - 1).astype(jnp.int32)
    conv_edges = jnp.where((back_pos >= 0)[:, :, None], mixer_signal[target], jnp.zeros((), jnp.bfloat16))
    return (mixed, last_states, conv_edges)
```

```python
import functools

import jax
import jax.numpy as jnp
from jax import lax
from jax.experimental import pallas as pl
from jax.experimental.pallas import tpu as pltpu
from jax.sharding import PartitionSpec as P

STRETCH = 64
BLOCKS = 8
LOG2E = 1.4426950408889634
F32 = jnp.float32
BF16 = jnp.bfloat16
HALO = 8


def placements(lengths_ref, order_ref):
    out = []
    position = jnp.int32(0)
    for i in range(lengths_ref.shape[0]):
        request = order_ref[i]
        length = lengths_ref[request]
        begin = position
        position = begin + (length + STRETCH - 1) // STRETCH * STRETCH
        out.append((request, begin, length, position))
    return out


def live_rows(laid, slots):
    live = jnp.zeros(slots.shape, jnp.bool_)
    for _, begin, length, _ in laid:
        live = live | ((slots >= begin) & (slots < begin + length))
    return live


def opens(laid, slots):
    hit = slots == laid[-1][3]
    for _, begin, _, _ in laid:
        hit = hit | (slots == begin)
    return hit


def norm_kernel(copies, tokens_ref, gain_ref, out_ref):
    wide = tokens_ref[...].astype(F32)
    scale = lax.rsqrt(jnp.mean(wide * wide, axis=1, keepdims=True) + 1e-05)
    normed = (wide * scale * gain_ref[...]).astype(BF16)
    for i in range(copies):
        out_ref[i] = normed


def entry_kernel(rows, lengths_ref, order_ref, own_ref, other_ref, weight_ref, inner_ref, gate_ref, tail_ref):
    core = lax.rem(lax.axis_index("chan"), 2)
    span = inner_ref.shape[0]
    base = lax.axis_index("seq") * span
    laid = placements(lengths_ref, order_ref)
    live = live_rows(laid, base + lax.broadcasted_iota(jnp.int32, (span, 1), 0))
    other = other_ref[...]
    first = core == 0
    arranged = []
    for k in range(2):
        own_part = own_ref[k]
        other_part = jnp.dot(other, weight_ref[k], preferred_element_type=F32)
        low = jnp.where(first, own_part, other_part)
        high = jnp.where(first, other_part, own_part)
        pieces = []
        for z in range(span // (2 * rows)):
            pieces += [low[z * rows : (z + 1) * rows], high[z * rows : (z + 1) * rows]]
        arranged.append(jnp.concatenate(pieces, axis=0))
    inner = jnp.where(live, arranged[0], 0.0)
    inner_ref[...] = inner.astype(BF16)
    tail_ref[...] = inner[span - HALO :].astype(BF16)
    gate = arranged[1].astype(BF16).astype(F32)
    gate_ref[...] = jnp.where(live, gate / (1.0 + jnp.exp(-gate)), 0.0)


def conv_kernel(lengths_ref, order_ref, inner_ref, halo_ref, taps_ref, bias_ref, wx_ref, act_ref, part_ref, edge_ref):
    span, width = inner_ref.shape
    base = lax.axis_index("seq") * span
    laid = placements(lengths_ref, order_ref)
    taps = taps_ref.shape[0]
    inner = inner_ref[...]
    wide = inner.astype(F32)
    before = halo_ref[...].astype(F32)
    for q in range(span // STRETCH):
        here = wide[q * STRETCH : (q + 1) * STRETCH]
        fresh = opens(laid, base + q * STRETCH)
        before = jnp.where(fresh, 0.0, before)
        extended = jnp.concatenate([before, here], axis=0)
        total = jnp.broadcast_to(bias_ref[...], here.shape)
        for k in range(taps - 1, -1, -1):
            shift = HALO - (taps - 1 - k)
            total = total + taps_ref[k : k + 1, :] * extended[shift : shift + STRETCH]
        act_ref[pl.ds(q * STRETCH, STRETCH), :] = (total / (1.0 + jnp.exp(-total))).astype(BF16)
        before = here[STRETCH - HALO :]
    part_ref[...] = jnp.dot(act_ref[...], wx_ref[...], preferred_element_type=F32).astype(BF16)
    column = lax.broadcasted_iota(jnp.int32, (1, 128), 1)
    target = jnp.full((1, 128), -1, jnp.int32)
    for request, begin, length, _ in laid:
        back = length - taps + (column - request * taps)
        mine = (column >= request * taps) & (column < request * taps + taps) & (back >= 0)
        target = jnp.where(mine, begin + back, target)
    slots = base + lax.broadcasted_iota(jnp.int32, (span, 128), 0)
    pick = (slots == target).astype(F32).astype(BF16)
    edge_ref[...] = lax.dot_general(inner, pick, (((0,), (0,)), ((), ())), preferred_element_type=F32)


def share_kernel(copies, parts_ref, out_ref):
    total = jnp.sum(parts_ref[...].astype(F32), axis=0).astype(BF16)
    for i in range(copies):
        out_ref[i] = total


def put(ref, values):
    for h in range(ref.shape[0]):
        ref[h] = values[:, h * 128 : (h + 1) * 128]


def every(ref, t, steps):
    return jnp.concatenate([ref[h, pl.ds(t, BLOCKS, stride=steps), :] for h in range(ref.shape[0])], axis=1)


def spread(values, n):
    return jnp.broadcast_to(values[:, n : n + 1], (BLOCKS, 128))


def twice(values, width):
    return jnp.concatenate([values] * (width // 128), axis=1)


def local_kernel(lengths_ref, order_ref, xp_ref, tm_ref, off_ref, act_ref, alog_ref, send_ref, delta_ref, drive_ref, rate_ref, coef_ref):
    span, width = act_ref.shape
    states = alog_ref.shape[0]
    rank = tm_ref.shape[0]
    steps = span // BLOCKS
    base = lax.axis_index("seq") * span
    laid = placements(lengths_ref, order_ref)
    live = live_rows(laid, base + lax.broadcasted_iota(jnp.int32, (span, 1), 0))
    xp = xp_ref[...]
    raw = jnp.dot(xp[:, :rank], tm_ref[...], preferred_element_type=F32) + off_ref[...]
    soft = jnp.maximum(raw, 0.0) + jnp.log1p(jnp.exp(-jnp.abs(raw)))
    delta = jnp.where(live, soft, 0.0)
    put(delta_ref, delta)
    put(drive_ref, delta * act_ref[...].astype(F32))
    coef = xp[:, rank:].astype(F32)
    coef_ref[...] = jnp.concatenate([coef, jnp.zeros((span, 128 - coef.shape[1]), F32)], axis=1)
    rate = -jnp.exp(alog_ref[...]) * LOG2E
    for n in range(states):
        rate_ref[n] = jnp.broadcast_to(rate[n : n + 1], (BLOCKS, width))

    def step(t, carry):
        total, state = carry
        now = every(delta_ref, t, steps)
        push = every(drive_ref, t, steps)
        coefs = coef_ref[pl.ds(t, BLOCKS, stride=steps), :]
        moved = []
        for n in range(states):
            moved.append(jnp.exp2(now * rate_ref[n]) * state[n] + push * twice(spread(coefs, n), width))
        return (total + now, tuple(moved))

    zero = jnp.zeros((BLOCKS, width), F32)
    total, state = lax.fori_loop(0, steps, step, (zero, (zero,) * states), unroll=2)
    dests, both, _ = send_ref.shape
    sub = both // 2
    send_ref[:, :sub, :] = jnp.concatenate(state, axis=0).T.reshape(dests, sub, states * BLOCKS)
    decay = [jnp.exp2(total * rate_ref[n]) for n in range(states)]
    send_ref[:, sub:, :] = jnp.concatenate(decay, axis=0).T.reshape(dests, sub, states * BLOCKS)


def chain_kernel(steps, lengths_ref, order_ref, got_ref, edge_ref, back_ref, last_ref, run_ref, tot_ref, all_ref, hold_ref):
    spans, both, lanes = got_ref.shape
    sub = both // 2
    states = lanes // BLOCKS
    laid = placements(lengths_ref, order_ref)
    block = lax.broadcasted_iota(jnp.int32, (1, 1, lanes), 2) % BLOCKS
    index = lax.broadcasted_iota(jnp.int32, (spans, 1, lanes), 0) * BLOCKS + block
    keep = jnp.where(opens(laid, index * steps), 0.0, 1.0)
    state = got_ref[:, :sub, :]
    decay = got_ref[:, sub:, :] * keep
    shift = 1
    while shift < BLOCKS:
        within = block >= shift
        prev_state = jnp.where(within, pltpu.roll(state, shift, 2), 0.0)
        prev_decay = jnp.where(within, pltpu.roll(decay, shift, 2), 1.0)
        state = state + decay * prev_state
        decay = decay * prev_decay
        shift *= 2

    def replicate(values):
        values = jnp.where(block == BLOCKS - 1, values, 0.0)
        shift = 1
        while shift < BLOCKS:
            values = values + pltpu.roll(values, lanes - shift, 2)
            shift *= 2
        return values

    run_ref[...] = replicate(state)
    tot_ref[...] = replicate(decay)
    entering = jnp.zeros((sub, lanes), F32)
    for s in range(spans):
        hold_ref[s] = entering
        entering = tot_ref[s] * entering + run_ref[s]
    held = hold_ref[...]
    ends = decay * held + state
    all_ref[...] = ends
    back_ref[:, :sub, :] = keep * jnp.where(block == 0, held, pltpu.roll(ends, 1, 2))
    back_ref[:, sub:, :] = edge_ref[...].reshape(spans, sub, lanes)
    row = lax.broadcasted_iota(jnp.int32, (states, lanes), 0)
    lane = lax.broadcasted_iota(jnp.int32, (states, lanes), 1)
    member = (lane // BLOCKS == row).astype(F32)
    lane_block = lax.broadcasted_iota(jnp.int32, (sub, lanes), 1) % BLOCKS
    for request, _, _, end in laid:
        final = end // steps - 1
        chosen = jnp.where(lane_block == final % BLOCKS, all_ref[final // BLOCKS], 0.0)
        last_ref[request] = lax.dot_general(
            member, chosen, (((1,), (1,)), ((), ())), precision=lax.Precision.HIGHEST, preferred_element_type=F32
        )


def output_kernel(rows, back_ref, delta_ref, drive_ref, rate_ref, coef_ref, act_ref, gate_ref, skip_ref, gated_ref, edge_ref, y_ref):
    span, width = act_ref.shape
    states = rate_ref.shape[0]
    steps = span // BLOCKS
    sources, both, lanes = back_ref.shape
    sub = both // 2
    core = lax.rem(lax.axis_index("chan"), 2)
    edge_ref[...] = jnp.sum(back_ref[:, sub:, :], axis=0)
    start = back_ref[:, :sub, :].reshape(sources * sub, lanes).T
    first = tuple(start[n * BLOCKS : (n + 1) * BLOCKS] for n in range(states))

    def step(t, state):
        now = every(delta_ref, t, steps)
        push = every(drive_ref, t, steps)
        coefs = coef_ref[pl.ds(t, BLOCKS, stride=steps), :]
        moved = []
        total = jnp.zeros((BLOCKS, width), F32)
        for n in range(states):
            after = jnp.exp2(now * rate_ref[n]) * state[n] + push * twice(spread(coefs, n), width)
            total = total + after * twice(spread(coefs, states + n), width)
            moved.append(after)
        for h in range(width // 128):
            y_ref[h, pl.ds(t, BLOCKS, stride=steps), :] = total[:, h * 128 : (h + 1) * 128]
        return tuple(moved)

    lax.fori_loop(0, steps, step, first, unroll=2)
    y = jnp.concatenate([y_ref[h] for h in range(width // 128)], axis=1)
    gated = (y + skip_ref[...] * act_ref[...].astype(F32)) * gate_ref[...]
    even, odd = [], []
    for z in range(span // (2 * rows)):
        even.append(gated[2 * z * rows : (2 * z + 1) * rows])
        odd.append(gated[(2 * z + 1) * rows : (2 * z + 2) * rows])
    even, odd = jnp.concatenate(even, axis=0), jnp.concatenate(odd, axis=0)
    mine = core == 0
    gated_ref[0] = jnp.where(mine, even, odd).astype(BF16)
    gated_ref[1] = jnp.where(mine, odd, even).astype(BF16)


def final_kernel(tokens_ref, parts_ref, out_ref):
    out_ref[...] = (tokens_ref[...].astype(F32) + jnp.sum(parts_ref[...].astype(F32), axis=0)).astype(BF16)


def call(kernel, name, out, *args, scalars=0, scratch=()):
    smem = [pl.BlockSpec(memory_space=pltpu.SMEM)] * scalars
    vmem = pl.BlockSpec(memory_space=pltpu.VMEM)
    shapes = [jax.ShapeDtypeStruct(*o) for o in out]
    result = pl.pallas_call(
        kernel,
        name=name,
        out_shape=shapes,
        in_specs=smem + [vmem] * (len(args) - scalars),
        out_specs=[vmem] * len(out),
        scratch_shapes=list(scratch),
    )(*args)
    return result if len(out) > 1 else result[0]


def on_device(
    tokens,
    norm_gain,
    entry_projection_matrix,
    conv_weight,
    conv_bias,
    w_x,
    timescale_matrix,
    timescale_offset,
    a_log,
    skip_gain,
    w_out,
    lengths,
    req_order,
):
    rows, model = tokens.shape
    chans, spans = lax.axis_size("chan"), lax.axis_size("seq")
    chips = chans // 2
    span = rows * chans
    width = entry_projection_matrix.shape[2]
    states = a_log.shape[0]
    cols = w_x.shape[1]
    reqs, taps = lengths.shape[0], conv_weight.shape[0]
    sub = width // spans
    lanes = states * BLOCKS
    parity = [[2 * z + k for z in range(chips)] for k in range(2)]
    partner = [(i, i ^ 1) for i in range(chans)]
    following = [(i, i + 1) for i in range(spans - 1)]

    def exchange(block, axis, groups=None):
        return lax.all_to_all(block, axis, 0, 0, axis_index_groups=groups)

    copies = call(functools.partial(norm_kernel, chips), "norm", [((chips, rows, model), BF16)], tokens, norm_gain[None])
    own = exchange(copies, "chan", parity).reshape(chips * rows, model)
    other = lax.ppermute(own, "chan", partner)
    own_part = jnp.einsum("td,kde->kte", own, entry_projection_matrix, preferred_element_type=F32)
    inner, gate, tail = call(
        functools.partial(entry_kernel, rows),
        "entry",
        [((span, width), BF16), ((span, width), F32), ((HALO, width), BF16)],
        lengths,
        req_order,
        own_part,
        other,
        entry_projection_matrix,
        scalars=2,
    )
    halo = lax.ppermute(tail, "seq", following)
    activated, part, edge = call(
        conv_kernel,
        "conv",
        [((span, width), BF16), ((span, cols), BF16), ((width, lanes), F32)],
        lengths,
        req_order,
        inner,
        halo,
        conv_weight,
        conv_bias[None],
        w_x,
        scalars=2,
    )
    parts = exchange(part.reshape(chans, rows, cols), "chan")
    summed = call(functools.partial(share_kernel, chans), "share", [((chans, rows, cols), BF16)], parts)
    x_proj = exchange(summed, "chan").reshape(span, cols)
    send, delta, drive, rate, coef = call(
        local_kernel,
        "local",
        [
            ((spans, 2 * sub, lanes), F32),
            ((width // 128, span, 128), F32),
            ((width // 128, span, 128), F32),
            ((states, BLOCKS, width), F32),
            ((span, 128), F32),
        ],
        lengths,
        req_order,
        x_proj,
        timescale_matrix,
        timescale_offset[None],
        activated,
        a_log,
        scalars=2,
    )
    got = exchange(send, "seq")
    back, last_states = call(
        functools.partial(chain_kernel, span // BLOCKS),
        "chain",
        [((spans, 2 * sub, lanes), F32), ((reqs, states, sub), F32)],
        lengths,
        req_order,
        got,
        edge,
        scalars=2,
        scratch=[pltpu.VMEM((spans, sub, lanes), F32)] * 4,
    )
    back = exchange(back, "seq")
    gated, edges = call(
        functools.partial(output_kernel, rows),
        "output",
        [((2, span // 2, width), BF16), ((sub, lanes), F32)],
        back,
        delta,
        drive,
        rate,
        coef,
        activated,
        gate,
        skip_gain[None],
        scratch=[pltpu.VMEM((width // 128, span, 128), F32)],
    )
    theirs = jnp.dot(gated[1], w_out, preferred_element_type=F32).astype(BF16)
    received = lax.ppermute(theirs, "chan", partner)
    ours = jnp.dot(gated[0], w_out, preferred_element_type=F32)
    pair = (ours + received.astype(F32)).astype(BF16).reshape(chips, rows, model)
    mixed = call(final_kernel, "final", [((rows, model), BF16)], tokens, exchange(pair, "chan", parity))
    conv_edges = edges[:, : reqs * taps].T.reshape(reqs, taps, sub).astype(BF16)
    return (mixed, last_states, conv_edges)


def solution(mesh):
    in_specs = (
        P(("seq", "chan"), None),
        P(),
        P(None, None, "chan"),
        P(None, "chan"),
        P("chan"),
        P("chan", None),
        P(None, "chan"),
        P("chan"),
        P(None, "chan"),
        P("chan"),
        P("chan", None),
        P(),
        P(),
    )
    out_specs = (
        P(("seq", "chan"), None),
        P(None, None, ("chan", "seq")),
        P(None, None, ("chan", "seq")),
    )
    return jax.shard_map(
        on_device, mesh=mesh, in_specs=in_specs, out_specs=out_specs, check_vma=False
    )
```

```python
import functools

import jax
import jax.numpy as jnp
from jax import lax
from jax.experimental import pallas as pl
from jax.experimental.pallas import tpu as pltpu
from jax.sharding import PartitionSpec as P

STRETCH = 64
BLOCKS = 8
LOG2E = 1.4426950408889634
F32 = jnp.float32
BF16 = jnp.bfloat16
HALO = 8
GRANT = 16 << 20


def placements(lengths_ref, order_ref):
    out = []
    position = jnp.int32(0)
    for i in range(lengths_ref.shape[0]):
        request = order_ref[i]
        length = lengths_ref[request]
        begin = position
        position = begin + (length + STRETCH - 1) // STRETCH * STRETCH
        out.append((request, begin, length, position))
    return out


def live_rows(laid, slots):
    live = jnp.zeros(slots.shape, jnp.bool_)
    for _, begin, length, _ in laid:
        live = live | ((slots >= begin) & (slots < begin + length))
    return live


def opens(laid, slots):
    hit = slots == laid[-1][3]
    for _, begin, _, _ in laid:
        hit = hit | (slots == begin)
    return hit


def norm_kernel(copies, tokens_ref, gain_ref, out_ref):
    wide = tokens_ref[...].astype(F32)
    scale = lax.rsqrt(jnp.mean(wide * wide, axis=1, keepdims=True) + 1e-05)
    normed = (wide * scale * gain_ref[...]).astype(BF16)
    for i in range(copies):
        out_ref[i] = normed


def entry_kernel(rows, lengths_ref, order_ref, own_ref, other_ref, weight_ref, inner_ref, gate_ref, tail_ref):
    core = lax.rem(lax.axis_index("chan"), 2)
    span = inner_ref.shape[0]
    base = lax.axis_index("seq") * span
    laid = placements(lengths_ref, order_ref)
    live = live_rows(laid, base + lax.broadcasted_iota(jnp.int32, (span, 1), 0))
    other = other_ref[...]
    first = core == 0
    arranged = []
    for k in range(2):
        own_part = own_ref[k]
        other_part = jnp.dot(other, weight_ref[k], preferred_element_type=F32)
        low = jnp.where(first, own_part, other_part)
        high = jnp.where(first, other_part, own_part)
        pieces = []
        for z in range(span // (2 * rows)):
            pieces += [low[z * rows : (z + 1) * rows], high[z * rows : (z + 1) * rows]]
        arranged.append(jnp.concatenate(pieces, axis=0))
    inner = jnp.where(live, arranged[0], 0.0)
    inner_ref[...] = inner.astype(BF16)
    tail_ref[...] = inner[span - HALO :].astype(BF16)
    gate = arranged[1].astype(BF16).astype(F32)
    gate_ref[...] = jnp.where(live, gate / (1.0 + jnp.exp(-gate)), 0.0)


def conv_kernel(lengths_ref, order_ref, inner_ref, halo_ref, taps_ref, bias_ref, wx_ref, act_ref, part_ref, edge_ref):
    span, width = inner_ref.shape
    base = lax.axis_index("seq") * span
    laid = placements(lengths_ref, order_ref)
    taps = taps_ref.shape[0]
    inner = inner_ref[...]
    wide = inner.astype(F32)
    before = halo_ref[...].astype(F32)
    for q in range(span // STRETCH):
        here = wide[q * STRETCH : (q + 1) * STRETCH]
        fresh = opens(laid, base + q * STRETCH)
        before = jnp.where(fresh, 0.0, before)
        extended = jnp.concatenate([before, here], axis=0)
        total = jnp.broadcast_to(bias_ref[...], here.shape)
        for k in range(taps - 1, -1, -1):
            shift = HALO - (taps - 1 - k)
            total = total + taps_ref[k : k + 1, :] * extended[shift : shift + STRETCH]
        act_ref[pl.ds(q * STRETCH, STRETCH), :] = (total / (1.0 + jnp.exp(-total))).astype(BF16)
        before = here[STRETCH - HALO :]
    part_ref[...] = lax.dot_general(
        act_ref[...], wx_ref[...], (((1,), (1,)), ((), ())), preferred_element_type=F32
    ).astype(BF16)
    column = lax.broadcasted_iota(jnp.int32, (1, 128), 1)
    target = jnp.full((1, 128), -1, jnp.int32)
    for request, begin, length, _ in laid:
        back = length - taps + (column - request * taps)
        mine = (column >= request * taps) & (column < request * taps + taps) & (back >= 0)
        target = jnp.where(mine, begin + back, target)
    slots = base + lax.broadcasted_iota(jnp.int32, (span, 128), 0)
    pick = (slots == target).astype(F32).astype(BF16)
    edges = lax.dot_general(inner, pick, (((0,), (0,)), ((), ())), preferred_element_type=F32)
    edge_ref[...] = edges.astype(BF16)


def share_kernel(copies, parts_ref, out_ref):
    total = jnp.sum(parts_ref[...].astype(F32), axis=0).astype(BF16)
    for i in range(copies):
        out_ref[i] = total


def put(ref, values):
    for h in range(ref.shape[0]):
        ref[h] = values[:, h * 128 : (h + 1) * 128]


def every(ref, t, steps):
    return jnp.concatenate([ref[h, pl.ds(t, BLOCKS, stride=steps), :] for h in range(ref.shape[0])], axis=1)


def spread(values, n):
    return jnp.broadcast_to(values[:, n : n + 1], (BLOCKS, 128))


def twice(values, width):
    return jnp.concatenate([values] * (width // 128), axis=1)


def local_kernel(lengths_ref, order_ref, xp_ref, tm_ref, off_ref, act_ref, alog_ref, send_ref, delta_ref, drive_ref, rate_ref, coef_ref):
    span, width = act_ref.shape
    states = alog_ref.shape[0]
    rank = tm_ref.shape[0]
    steps = span // BLOCKS
    base = lax.axis_index("seq") * span
    laid = placements(lengths_ref, order_ref)
    live = live_rows(laid, base + lax.broadcasted_iota(jnp.int32, (span, 1), 0))
    xp = xp_ref[...]
    raw = jnp.dot(xp[:, :rank], tm_ref[...], preferred_element_type=F32) + off_ref[...]
    soft = jnp.maximum(raw, 0.0) + jnp.log1p(jnp.exp(-jnp.abs(raw)))
    delta = jnp.where(live, soft, 0.0)
    put(delta_ref, delta)
    put(drive_ref, delta * act_ref[...].astype(F32))
    coef = xp[:, rank:].astype(F32)
    coef_ref[...] = jnp.concatenate([coef, jnp.zeros((span, 128 - coef.shape[1]), F32)], axis=1)
    rate = -jnp.exp(alog_ref[...]) * LOG2E
    for n in range(states):
        rate_ref[n] = jnp.broadcast_to(rate[n : n + 1], (BLOCKS, width))

    def step(t, carry):
        total, state = carry
        now = every(delta_ref, t, steps)
        push = every(drive_ref, t, steps)
        coefs = coef_ref[pl.ds(t, BLOCKS, stride=steps), :]
        moved = []
        for n in range(states):
            moved.append(jnp.exp2(now * rate_ref[n]) * state[n] + push * twice(spread(coefs, n), width))
        return (total + now, tuple(moved))

    zero = jnp.zeros((BLOCKS, width), F32)
    total, state = lax.fori_loop(0, steps, step, (zero, (zero,) * states), unroll=2)
    dests, both, lanes = send_ref.shape
    sub = both // 2
    send_ref[:, :sub, :] = jnp.concatenate(state, axis=0).T.reshape(dests, sub, lanes).astype(BF16)
    terms = []
    for _ in range(3):
        term = total.astype(BF16).astype(F32)
        terms.append(term)
        total = total - term
    terms.append(jnp.zeros((lanes - 3 * BLOCKS, width), F32))
    send_ref[:, sub:, :] = jnp.concatenate(terms, axis=0).T.reshape(dests, sub, lanes).astype(BF16)


def chain_kernel(steps, lengths_ref, order_ref, got_ref, edge_ref, alog_ref, back_ref, last_ref, rate_ref, run_ref, tot_ref, all_ref, hold_ref):
    spans, both, lanes = got_ref.shape
    sub = both // 2
    states = lanes // BLOCKS
    laid = placements(lengths_ref, order_ref)
    block = lax.broadcasted_iota(jnp.int32, (1, 1, lanes), 2) % BLOCKS
    index = lax.broadcasted_iota(jnp.int32, (spans, 1, lanes), 0) * BLOCKS + block
    keep = jnp.where(opens(laid, index * steps), 0.0, 1.0)
    row = lax.broadcasted_iota(jnp.int32, (states, lanes), 0)
    lane = lax.broadcasted_iota(jnp.int32, (states, lanes), 1)
    member = (lane // BLOCKS == row).astype(F32)
    rate = -jnp.exp(alog_ref[...]) * LOG2E
    rate_ref[...] = lax.dot_general(
        rate, member, (((0,), (0,)), ((), ())), precision=lax.Precision.HIGHEST, preferred_element_type=F32
    )
    mine = rate_ref[pl.ds(pl.multiple_of(lax.axis_index("seq") * sub, sub), sub), :]
    source = lax.broadcasted_iota(jnp.int32, (lanes, lanes), 0)
    target = lax.broadcasted_iota(jnp.int32, (lanes, lanes), 1)
    gather = ((source % BLOCKS == target % BLOCKS) & (source < 3 * BLOCKS)).astype(F32).astype(BF16)
    sums = jnp.dot(got_ref[:, sub:, :].reshape(spans * sub, lanes), gather, preferred_element_type=F32)
    state = got_ref[:, :sub, :].astype(F32)
    decay = jnp.exp2(sums.reshape(spans, sub, lanes) * mine[None]) * keep
    shift = 1
    while shift < BLOCKS:
        within = block >= shift
        prev_state = jnp.where(within, pltpu.roll(state, shift, 2), 0.0)
        prev_decay = jnp.where(within, pltpu.roll(decay, shift, 2), 1.0)
        state = state + decay * prev_state
        decay = decay * prev_decay
        shift *= 2

    def replicate(values):
        values = jnp.where(block == BLOCKS - 1, values, 0.0)
        shift = 1
        while shift < BLOCKS:
            values = values + pltpu.roll(values, lanes - shift, 2)
            shift *= 2
        return values

    run_ref[...] = replicate(state)
    tot_ref[...] = replicate(decay)
    entering = jnp.zeros((sub, lanes), F32)
    for s in range(spans):
        hold_ref[s] = entering
        entering = tot_ref[s] * entering + run_ref[s]
    held = hold_ref[...]
    ends = decay * held + state
    all_ref[...] = ends
    back_ref[:, :sub, :] = (keep * jnp.where(block == 0, held, pltpu.roll(ends, 1, 2))).astype(BF16)
    back_ref[:, sub:, :] = edge_ref[...].reshape(spans, sub, lanes)
    lane_block = lax.broadcasted_iota(jnp.int32, (sub, lanes), 1) % BLOCKS
    for request, _, _, end in laid:
        final = end // steps - 1
        chosen = jnp.where(lane_block == final % BLOCKS, all_ref[final // BLOCKS], 0.0)
        last_ref[request] = lax.dot_general(
            chosen, member, (((1,), (1,)), ((), ())), precision=lax.Precision.HIGHEST, preferred_element_type=F32
        )


def output_kernel(rows, back_ref, delta_ref, drive_ref, rate_ref, coef_ref, act_ref, gate_ref, skip_ref, wout_ref, gated_ref, theirs_ref, edge_ref, y_ref):
    span, width = act_ref.shape
    states = rate_ref.shape[0]
    steps = span // BLOCKS
    sources, both, lanes = back_ref.shape
    sub = both // 2
    core = lax.rem(lax.axis_index("chan"), 2)
    edge_ref[...] = jnp.sum(back_ref[:, sub:, :].astype(F32), axis=0)
    start = back_ref[:, :sub, :].astype(F32).reshape(sources * sub, lanes).T
    first = tuple(start[n * BLOCKS : (n + 1) * BLOCKS] for n in range(states))

    def step(t, state):
        now = every(delta_ref, t, steps)
        push = every(drive_ref, t, steps)
        coefs = coef_ref[pl.ds(t, BLOCKS, stride=steps), :]
        moved = []
        total = jnp.zeros((BLOCKS, width), F32)
        for n in range(states):
            after = jnp.exp2(now * rate_ref[n]) * state[n] + push * twice(spread(coefs, n), width)
            total = total + after * twice(spread(coefs, states + n), width)
            moved.append(after)
        for h in range(width // 128):
            y_ref[h, pl.ds(t, BLOCKS, stride=steps), :] = total[:, h * 128 : (h + 1) * 128]
        return tuple(moved)

    lax.fori_loop(0, steps, step, first, unroll=2)
    y = jnp.concatenate([y_ref[h] for h in range(width // 128)], axis=1)
    gated = (y + skip_ref[...] * act_ref[...].astype(F32)) * gate_ref[...]
    even, odd = [], []
    for z in range(span // (2 * rows)):
        even.append(gated[2 * z * rows : (2 * z + 1) * rows])
        odd.append(gated[(2 * z + 1) * rows : (2 * z + 2) * rows])
    even, odd = jnp.concatenate(even, axis=0), jnp.concatenate(odd, axis=0)
    mine = core == 0
    gated_ref[...] = jnp.where(mine, even, odd).astype(BF16)
    away = jnp.where(mine, odd, even).astype(BF16)
    theirs_ref[...] = jnp.dot(away, wout_ref[...], preferred_element_type=F32).astype(BF16)


def final_kernel(tokens_ref, parts_ref, out_ref):
    out_ref[...] = (tokens_ref[...].astype(F32) + jnp.sum(parts_ref[...].astype(F32), axis=0)).astype(BF16)


def call(kernel, name, out, *args, scalars=0, scratch=()):
    smem = [pl.BlockSpec(memory_space=pltpu.SMEM)] * scalars
    vmem = pl.BlockSpec(memory_space=pltpu.VMEM)
    shapes = [jax.ShapeDtypeStruct(*o) if name == "final" else pltpu.VMEM(*o) for o in out]
    args = args[:scalars] + tuple(pltpu.with_memory_space_constraint(a, pltpu.VMEM) for a in args[scalars:])
    result = pl.pallas_call(
        kernel,
        name=name,
        out_shape=shapes,
        in_specs=smem + [vmem] * (len(args) - scalars),
        out_specs=[vmem] * len(out),
        scratch_shapes=list(scratch),
        compiler_params=pltpu.CompilerParams(vmem_limit_bytes=GRANT),
    )(*args)
    return result if len(out) > 1 else result[0]


def on_device(
    tokens,
    norm_gain,
    entry_projection_matrix,
    conv_weight,
    conv_bias,
    w_x,
    timescale_matrix,
    timescale_offset,
    a_log,
    skip_gain,
    w_out,
    lengths,
    req_order,
):
    rows, model = tokens.shape
    chans, spans = lax.axis_size("chan"), lax.axis_size("seq")
    chips = chans // 2
    span = rows * chans
    width = entry_projection_matrix.shape[2]
    states = a_log.shape[0]
    cols = w_x.shape[1]
    reqs, taps = lengths.shape[0], conv_weight.shape[0]
    sub = width // spans
    lanes = states * BLOCKS
    parity = [[2 * z + k for z in range(chips)] for k in range(2)]
    partner = [(i, i ^ 1) for i in range(chans)]
    following = [(i, i + 1) for i in range(spans - 1)]

    def exchange(block, axis, groups=None):
        return lax.all_to_all(block, axis, 0, 0, axis_index_groups=groups)

    copies = call(functools.partial(norm_kernel, chips), "norm", [((chips, rows, model), BF16)], tokens, norm_gain[None])
    own = exchange(copies, "chan", parity).reshape(chips * rows, model)
    other = lax.ppermute(own, "chan", partner)
    own_part = jnp.einsum("td,kde->kte", own, entry_projection_matrix, preferred_element_type=F32)
    inner, gate, tail = call(
        functools.partial(entry_kernel, rows),
        "entry",
        [((span, width), BF16), ((span, width), F32), ((HALO, width), BF16)],
        lengths,
        req_order,
        own_part,
        other,
        entry_projection_matrix,
        scalars=2,
    )
    halo = lax.ppermute(tail, "seq", following)
    activated, part, edge = call(
        conv_kernel,
        "conv",
        [((span, width), BF16), ((span, cols), BF16), ((width, lanes), BF16)],
        lengths,
        req_order,
        inner,
        halo,
        conv_weight,
        conv_bias[None],
        w_x.T,
        scalars=2,
    )
    parts = exchange(part.reshape(chans, rows, cols), "chan")
    summed = call(functools.partial(share_kernel, chans), "share", [((chans, rows, cols), BF16)], parts)
    x_proj = exchange(summed, "chan").reshape(span, cols)
    send, delta, drive, rate, coef = call(
        local_kernel,
        "local",
        [
            ((spans, 2 * sub, lanes), BF16),
            ((width // 128, span, 128), F32),
            ((width // 128, span, 128), F32),
            ((states, BLOCKS, width), F32),
            ((span, 128), F32),
        ],
        lengths,
        req_order,
        x_proj,
        timescale_matrix,
        timescale_offset[None],
        activated,
        a_log,
        scalars=2,
    )
    got = exchange(send, "seq")
    back, last_states = call(
        functools.partial(chain_kernel, span // BLOCKS),
        "chain",
        [((spans, 2 * sub, lanes), BF16), ((reqs, sub, states), F32)],
        lengths,
        req_order,
        got,
        edge,
        a_log,
        scalars=2,
        scratch=[pltpu.VMEM((width, lanes), F32)] + [pltpu.VMEM((spans, sub, lanes), F32)] * 4,
    )
    back = exchange(back, "seq")
    gated, theirs, edges = call(
        functools.partial(output_kernel, rows),
        "output",
        [((span // 2, width), BF16), ((span // 2, model), BF16), ((sub, lanes), F32)],
        back,
        delta,
        drive,
        rate,
        coef,
        activated,
        gate,
        skip_gain[None],
        w_out,
        scratch=[pltpu.VMEM((width // 128, span, 128), F32)],
    )
    received = lax.ppermute(theirs, "chan", partner)
    ours = lax.optimization_barrier(jnp.dot(gated, w_out, preferred_element_type=F32))
    pair = (ours + received.astype(F32)).astype(BF16).reshape(chips, rows, model)
    mixed = call(final_kernel, "final", [((rows, model), BF16)], tokens, exchange(pair, "chan", parity))
    conv_edges = edges[:, : reqs * taps].T.reshape(reqs, taps, sub).astype(BF16)
    return (mixed, jnp.swapaxes(last_states, 1, 2), conv_edges)


def solution(mesh):
    in_specs = (
        P(("seq", "chan"), None),
        P(),
        P(None, None, "chan"),
        P(None, "chan"),
        P("chan"),
        P("chan", None),
        P(None, "chan"),
        P("chan"),
        P(None, "chan"),
        P("chan"),
        P("chan", None),
        P(),
        P(),
    )
    out_specs = (
        P(("seq", "chan"), None),
        P(None, None, ("chan", "seq")),
        P(None, None, ("chan", "seq")),
    )
    return jax.shard_map(
        on_device, mesh=mesh, in_specs=in_specs, out_specs=out_specs, check_vma=False
    )
```
